32 devices in a mesh: groups: 2 (over y), frame: 4 (over z), head: 2 (over x), seq: 2 (over core).
Axes of the slice: x: 2, y: 2, z: 4, core: 2. Of those that a mesh axis runs over, the one named last changes fastest.
Arguments:
- queries: bfloat16 [32, 1024, 1280], P(('groups', 'frame'), 'seq', 'head'), parts along dimension 0, may hold values from -240 to 240
- key_states: bfloat16 [32, 1024, 1280], P(('groups', 'frame'), 'seq', 'head'), parts along dimension 0, may hold values from -6.5 to 6.5
- value_states: bfloat16 [32, 1024, 1280], P(('groups', 'frame'), 'seq', 'head'), parts along dimension 0, may hold values from -6 to 6
Outputs:
- attended: bfloat16 [32, 1024, 1280], P(('groups', 'frame'), 'seq', 'head'), parts along dimension 0
The draws below stay inside these ranges and needn't reach their ends.
There are 2 independent parts, one for each index of `groups`. The reference program is written for one: setup_inputs(seed, part) draws one part's arguments, and reference() takes and returns one part's arrays. A program takes and returns all parts, laid end to end along the dimension named above; each array names one. Nothing has to cross between parts.
All inputs are finite; a program needn't handle non-finite values.
Results may differ from the reference program's by a relative error of at most 0.0075.
Values may be sent and summed in bfloat16 or wider, within the bound.
A program may use at most 128 MiB of HBM per device.

```python
import jax
import jax.numpy as jnp
from jax import lax

HEAD_DIM = 64
FRAME_TOK = 1024
FRAMES = 16
WIDTH = 1280


def shared_keys(key):
    drawn = jax.random.normal(jax.random.fold_in(key, 7), (FRAMES, FRAME_TOK, WIDTH), jnp.float32)
    return jnp.clip(drawn, -6.0, 6.0)


def draw_key_states(key, part):
    key_values = shared_keys(key)
    return key_values.astype(jnp.bfloat16)


def draw_queries(key, part):
    shape = (FRAMES, FRAME_TOK, WIDTH)
    drawn = jnp.clip(jax.random.normal(jax.random.fold_in(key, 11), shape, jnp.float32), -6.0, 6.0)
    return drawn.astype(jnp.bfloat16)


def steps_of(rng, shape, pieces, low, high):
    factor_of = 1.0
    for position, parts in pieces:
        draws = jax.random.uniform(jax.random.fold_in(jax.random.fold_in(rng, 6), position), (parts,), jnp.float32, low / len(pieces), high / len(pieces))
        factor_of = factor_of * jnp.repeat(jnp.exp(draws), shape[position] // parts).reshape((-1,) + (1,) * (len(shape) - 1 - position))
    return factor_of


def normal_values(rng, shape, scale, bound, cuts=(), kind=jnp.bfloat16):
    result = scale * jax.random.normal(rng, shape, jnp.float32)
    if cuts:
        result = result * steps_of(rng, shape, cuts, -0.22, 0.18)
    return jnp.clip(result, -bound, bound).astype(kind)


def setup_inputs(seed: int = 0, part: int = 0) -> dict:
    arg_keys = jax.random.split(jax.random.key(seed), 4)
    part_splits = jax.random.split(jax.random.fold_in(arg_keys[3], part), 4)
    return {
        "queries": draw_queries(jax.random.fold_in(jax.random.fold_in(arg_keys[3], part), 71), part),
        "key_states": draw_key_states(jax.random.fold_in(jax.random.fold_in(arg_keys[3], part), 71), part),
        "value_states": normal_values(part_splits[2], (FRAMES, FRAME_TOK, WIDTH), 1.0, 6.0, ((0, 4), (1, 2), (2, 2))),
    }


def attend(query_rows, key_rows, value_rows):
    row_count = query_rows.shape[0]
    head_count = query_rows.shape[1] // HEAD_DIM
    query_heads = query_rows.reshape(row_count, head_count, HEAD_DIM).astype(jnp.float32)
    key_heads = key_rows.reshape(key_rows.shape[0], head_count, HEAD_DIM).astype(jnp.float32)
    value_heads = value_rows.reshape(value_rows.shape[0], head_count, HEAD_DIM).astype(jnp.float32)
    scores = jnp.einsum("rhd,khd->hrk", query_heads, key_heads) * (HEAD_DIM ** -0.5)
    row_max = jnp.max(scores, axis=2, keepdims=True)
    weights = jnp.exp(scores - row_max)
    row_sum = jnp.sum(weights, axis=2, keepdims=True)
    rounded = weights.astype(jnp.bfloat16).astype(jnp.float32)
    outputs = jnp.einsum("hrk,khd->hrd", rounded, value_heads) / row_sum
    return outputs.transpose(1, 0, 2).reshape(row_count, head_count * HEAD_DIM).astype(jnp.bfloat16)


def reference(queries, key_states, value_states):
    def one_frame(frame_idx):
        prior_idx = jnp.maximum(frame_idx - 1, 0).astype(jnp.int32)
        key_set = jnp.concatenate([key_states[0], lax.dynamic_index_in_dim(key_states, prior_idx, 0, False)], 0)
        value_set = jnp.concatenate([value_states[0], lax.dynamic_index_in_dim(value_states, prior_idx, 0, False)], 0)
        query_now = lax.dynamic_index_in_dim(queries, frame_idx, 0, False)
        return attend(query_now, key_set, value_set)

    return lax.map(one_frame, jnp.arange(FRAMES, dtype=jnp.int32))
```

```python
import jax
import jax.numpy as jnp
from jax import lax
from jax.experimental import pallas as pl
from jax.experimental.pallas import tpu as pltpu
from jax.sharding import PartitionSpec as P

HEAD_DIM = 64
LANES = 128


def from_behind(value, axis, steps):
    count = lax.axis_size(axis)
    first, last = (max(0, -steps), min(count, count - steps))
    return lax.ppermute(value, axis, [(source, source + steps) for source in range(first, last)])


def spread(x, axis, root):
    mine = lax.axis_index(axis) == root
    return lax.psum(jnp.where(mine, x, jnp.zeros_like(x)), axis)


def attend_columns(q, keys, values):
    width = q.shape[1]
    head_of_lane = lax.broadcasted_iota(jnp.int32, q.shape, 1) // HEAD_DIM
    scaled = q * jnp.asarray(HEAD_DIM**-0.5, q.dtype)
    summed = [jnp.concatenate([v, jnp.ones_like(v)], 1) for v in values]
    result = None
    for head in range(width // HEAD_DIM):
        one = jnp.where(head_of_lane == head, scaled, jnp.zeros_like(scaled))
        scores = [
            lax.dot_general(one, k, (((1,), (1,)), ((), ())), preferred_element_type=jnp.float32)
            for k in keys
        ]
        row_max = jnp.max(scores[0], axis=1, keepdims=True)
        for s in scores[1:]:
            row_max = jnp.maximum(row_max, jnp.max(s, axis=1, keepdims=True))
        total = None
        for s, v in zip(scores, summed):
            rounded = jnp.exp(s - row_max).astype(jnp.bfloat16)
            part = jnp.dot(rounded, v, preferred_element_type=jnp.float32)
            total = part if total is None else total + part
        out = total[:, :width] / total[:, width:]
        result = out if result is None else jnp.where(head_of_lane == head, out, result)
    return result.astype(jnp.bfloat16)


def frame_kernel(q_ref, ka_ref, va_ref, kp_ref, vp_ref, o_ref):
    rows, columns = q_ref.shape[1:]
    block = min(rows, 256)

    def one(first, width, row):
        at = pl.ds(first, width)
        rows_at = pl.ds(pl.multiple_of(row * block, block), block)
        o_ref[0, rows_at, at] = attend_columns(
            q_ref[0, rows_at, at],
            [ka_ref[:, at], kp_ref[0, :, at]],
            [va_ref[:, at], vp_ref[0, :, at]],
        )

    pairs = columns // LANES
    blocks = rows // block

    @pl.loop(0, pairs * blocks)
    def _(step):
        one(pl.multiple_of((step // blocks) * LANES, LANES), LANES, step % blocks)

    if columns % LANES:

        @pl.loop(0, blocks)
        def _(step):
            one(pairs * LANES, columns % LANES, step)


def local(queries, key_states, value_states):
    frames, rows, columns = queries.shape
    at_root = lax.axis_index("frame") == 0
    key_value = jnp.stack([key_states, value_states], 0)
    whole = lax.all_gather(key_value, "seq", axis=2, tiled=True)
    shifted = from_behind(whole[:, frames - 1], "frame", 1)
    anchor = spread(whole[:, 0], "frame", 0)
    prior = jnp.where(at_root, anchor, shifted)
    previous = jnp.concatenate([prior[:, None], whole[:, : frames - 1]], 1)
    tokens = whole.shape[2]
    mine = pl.BlockSpec((1, rows, columns), lambda f: (f, 0, 0))
    first = pl.BlockSpec((tokens, columns), lambda f: (0, 0))
    before = pl.BlockSpec((1, tokens, columns), lambda f: (f, 0, 0))
    return pl.pallas_call(
        frame_kernel,
        grid=(frames,),
        out_shape=jax.ShapeDtypeStruct(queries.shape, queries.dtype),
        in_specs=[mine, first, first, before, before],
        out_specs=mine,
        compiler_params=pltpu.CompilerParams(vmem_limit_bytes=48 * 1024 * 1024),
    )(queries, anchor[0], anchor[1], previous[0], previous[1])


def solution(mesh):
    spec = P(("groups", "frame"), "seq", "head")
    return jax.shard_map(
        local, mesh=mesh, in_specs=(spec, spec, spec), out_specs=spec, check_vma=False
    )
```

```python
import functools

import jax
import jax.numpy as jnp
from jax import lax
from jax.experimental import pallas as pl
from jax.experimental.pallas import tpu as pltpu
from jax.sharding import PartitionSpec as P

HEAD_DIM = 64
LANES = 128


def attend_columns(q, keys, values):
    width = q.shape[1]
    head_of_lane = lax.broadcasted_iota(jnp.int32, q.shape, 1) // HEAD_DIM
    scaled = q * jnp.asarray(HEAD_DIM**-0.5, q.dtype)
    summed = [jnp.concatenate([v, jnp.ones_like(v)], 1) for v in values]
    result = None
    for head in range(width // HEAD_DIM):
        one = jnp.where(head_of_lane == head, scaled, jnp.zeros_like(scaled))
        scores = [
            lax.dot_general(one, k, (((1,), (1,)), ((), ())), preferred_element_type=jnp.float32)
            for k in keys
        ]
        row_max = jnp.max(scores[0], axis=1, keepdims=True)
        for s in scores[1:]:
            row_max = jnp.maximum(row_max, jnp.max(s, axis=1, keepdims=True))
        total = None
        for s, v in zip(scores, summed):
            rounded = jnp.exp(s - row_max).astype(jnp.bfloat16)
            part = jnp.dot(rounded, v, preferred_element_type=jnp.float32)
            total = part if total is None else total + part
        out = total[:, :width] / total[:, width:]
        result = out if result is None else jnp.where(head_of_lane == head, out, result)
    return result.astype(jnp.bfloat16)


def kernel(
    blocks,
    halves,
    q_ref,
    k_ref,
    v_ref,
    o_ref,
    k_buf,
    v_buf,
    own_sem,
    swap_send,
    swap_recv,
    prior_send,
    prior_recv,
    anchor_send,
    anchor_recv,
    relay_send,
    relay_recv,
):
    frames, rows, columns = q_ref.shape
    chunks = own_sem.shape[1]
    width = columns // chunks
    anchor_slot, prior_slot = frames, frames + 1
    z = lax.axis_index("frame")
    half = lax.axis_index("seq")
    later = (z + blocks - 1) // blocks
    ahead = {"frame": (z + 1) % blocks}
    first = z == 0
    sends_on = z < blocks - 1
    mine = pl.ds(pl.multiple_of(half * rows, rows), rows)
    sources, buffers = (k_ref, v_ref), (k_buf, v_buf)
    offsets = range(1, halves)

    def cols(c):
        return pl.ds(pl.multiple_of(c * width, LANES), width) if chunks > 1 else pl.ds(0, width)

    def sibling(j):
        return {"seq": (half + j) % halves}

    def remote(src, dst, send, recv, where):
        return pltpu.make_async_remote_copy(
            src_ref=src,
            dst_ref=dst,
            send_sem=send,
            recv_sem=recv,
            device_id=where,
            device_id_type=pl.DeviceIdType.MESH,
        )

    def own(i, c):
        return pltpu.make_async_copy(
            sources[i].at[pl.ds(0, frames - 1), :, cols(c)],
            buffers[i].at[pl.ds(0, frames - 1), mine, cols(c)],
            own_sem.at[i, c],
        )

    def swap(i, c, j):
        return remote(
            sources[i].at[pl.ds(0, frames - 1), :, cols(c)],
            buffers[i].at[pl.ds(0, frames - 1), mine, cols(c)],
            swap_send.at[i, c, j - 1],
            swap_recv.at[i, c, j - 1],
            sibling(j),
        )

    def prior(i, c):
        return remote(
            sources[i].at[frames - 1, :, cols(c)],
            buffers[i].at[prior_slot, mine, cols(c)],
            prior_send.at[i, c],
            prior_recv.at[i, c],
            ahead,
        )

    def anchor(i, c, root):
        here = buffers[i].at[anchor_slot, mine, cols(c)]
        return remote(
            sources[i].at[0, :, cols(c)] if root else here,
            here,
            anchor_send.at[i, c],
            anchor_recv.at[i, c],
            ahead,
        )

    def relay(which, i, c, j):
        here = buffers[i].at[anchor_slot + which, mine, cols(c)]
        return remote(
            here,
            here,
            relay_send.at[which, i, c, j - 1],
            relay_recv.at[which, i, c, j - 1],
            sibling(j),
        )

    barrier = pltpu.get_barrier_semaphore()

    @pl.when(sends_on)
    def _():
        pl.semaphore_signal(
            barrier, inc=1, device_id=ahead, device_id_type=pl.DeviceIdType.MESH
        )

    @pl.when(z > 0)
    def _():
        pl.semaphore_signal(
            barrier,
            inc=1,
            device_id={"frame": (z + blocks - 1) % blocks},
            device_id_type=pl.DeviceIdType.MESH,
        )

    for j in offsets:
        pl.semaphore_signal(
            barrier, inc=1, device_id=sibling(j), device_id_type=pl.DeviceIdType.MESH
        )
    pl.semaphore_wait(barrier, later + 1 - (z + 1) // blocks + halves - 1)

    @pl.when(first & sends_on)
    def _():
        @pl.loop(0, chunks)
        def _(c):
            for i in range(2):
                anchor(i, c, True).start()
            for i in range(2):
                prior(i, c).start()

    @pl.when((z > 0) & sends_on)
    def _():
        for i in range(2):
            prior(i, 0).start()

    @pl.loop(0, chunks)
    def _(c):
        for i in range(2):
            own(i, c).start()
            for j in offsets:
                swap(i, c, j).start()

    def receive(c):
        @pl.when(z > 0)
        def _():
            for i in range(2):
                anchor(i, c, False).wait_recv()

                @pl.when(sends_on)
                def _():
                    anchor(i, c, False).start()

                for j in offsets:
                    relay(0, i, c, j).start()

            @pl.when(sends_on & (c + 1 < chunks))
            def _():
                for i in range(2):
                    prior(i, c + 1).start()

            for i in range(2):
                prior(i, c).wait_recv()
                for j in offsets:
                    relay(1, i, c, j).start()

    def complete(c):
        for i in range(2):
            own(i, c).wait()
            for j in offsets:
                swap(i, c, j).wait_recv()

        @pl.when(z > 0)
        def _():
            for i in range(2):
                for j in offsets:
                    relay(0, i, c, j).wait_recv()
                    relay(1, i, c, j).wait_recv()

    block = min(rows, 256)
    per_frame = rows // block
    steps = frames * per_frame

    def compute(c, step):
        frame = step // per_frame
        opens = (frames - frame) // frames
        before = (frame - 1) * (1 - opens) + opens * later * prior_slot
        zero = later * anchor_slot
        at_rows = pl.ds(pl.multiple_of((step % per_frame) * block, block), block)
        for start in range(0, width, LANES):
            size = min(LANES, width - start)
            if chunks > 1:
                at = cols(c)
            else:
                at = pl.ds(start, size)
            o_ref[frame, at_rows, at] = attend_columns(
                q_ref[frame, at_rows, at],
                [k_buf[zero, :, at], k_buf[before, :, at]],
                [v_buf[zero, :, at], v_buf[before, :, at]],
            )

    receive(0)

    @pl.loop(0, chunks)
    def _(c):
        complete(c)

        @pl.loop(0, steps)
        def _(step):
            @pl.when((step == steps // 2) & (c + 1 < chunks))
            def _():
                receive(c + 1)

            compute(c, step)

    @pl.loop(0, chunks)
    def _(c):
        for i in range(2):
            for j in offsets:
                swap(i, c, j).wait_send()

            @pl.when(sends_on)
            def _():
                prior(i, c).wait_send()
                anchor(i, c, False).wait_send()

            @pl.when(z > 0)
            def _():
                for j in offsets:
                    relay(0, i, c, j).wait_send()
                    relay(1, i, c, j).wait_send()


def local(blocks, halves, queries, key_states, value_states):
    frames, rows, columns = queries.shape
    chunks = columns // LANES if columns % LANES == 0 else 1
    held = pltpu.VMEM((frames + 2, rows * halves, columns), queries.dtype)
    dma = pltpu.SemaphoreType.DMA
    plain = dma((2, chunks))
    across = dma((2, chunks, halves - 1))
    relays = dma((2, 2, chunks, halves - 1))
    anywhere = pl.BlockSpec(memory_space=pl.ANY)
    near = pl.BlockSpec(memory_space=pltpu.VMEM)
    return pl.pallas_call(
        functools.partial(kernel, blocks, halves),
        out_shape=jax.ShapeDtypeStruct(queries.shape, queries.dtype),
        in_specs=[near, anywhere, anywhere],
        out_specs=near,
        scratch_shapes=[
            held,
            held,
            plain,
            across,
            across,
            plain,
            plain,
            plain,
            plain,
            relays,
            relays,
        ],
        compiler_params=pltpu.CompilerParams(
            collective_id=0, has_side_effects=True, vmem_limit_bytes=56 * 1024 * 1024
        ),
    )(queries, key_states, value_states)


def solution(mesh):
    spec = P(("groups", "frame"), "seq", "head")
    body = functools.partial(local, mesh.shape["frame"], mesh.shape["seq"])
    return jax.shard_map(
        body, mesh=mesh, in_specs=(spec, spec, spec), out_specs=spec, check_vma=False
    )
```

```python
import functools

import jax
import jax.numpy as jnp
from jax import lax
from jax.experimental import pallas as pl
from jax.experimental.pallas import tpu as pltpu
from jax.sharding import PartitionSpec as P

HEAD_DIM = 64
LANES = 128
KEY_BLOCK = 512


def attend_columns(q, keys, values):
    rows, width = q.shape
    heads = width // HEAD_DIM
    head_of_lane = lax.broadcasted_iota(jnp.int32, q.shape, 1) // HEAD_DIM
    scaled = q * jnp.asarray(HEAD_DIM**-0.5, q.dtype)
    stacked = jnp.concatenate(
        [jnp.where(head_of_lane == h, scaled, jnp.zeros_like(scaled)) for h in range(heads)], 0
    )
    row_max = total = None
    for k, v in zip(keys, values):
        for start in range(0, k.shape[0], KEY_BLOCK):
            k_part, v_part = k[start : start + KEY_BLOCK], v[start : start + KEY_BLOCK]
            summed = jnp.concatenate([v_part, jnp.ones_like(v_part)], 1)
            scores = lax.dot_general(
                stacked, k_part, (((1,), (1,)), ((), ())), preferred_element_type=jnp.float32
            )
            newer = jnp.max(scores, axis=1, keepdims=True)
            if row_max is not None:
                newer = jnp.maximum(row_max, newer)
            rounded = jnp.exp(scores - newer).astype(jnp.bfloat16)
            part = jnp.dot(rounded, summed, preferred_element_type=jnp.float32)
            total = part if row_max is None else total * jnp.exp(row_max - newer) + part
            row_max = newer
    out = total[:, :width] / total[:, width:]
    result = out[:rows]
    for h in range(1, heads):
        result = jnp.where(head_of_lane == h, out[h * rows : (h + 1) * rows], result)
    return result.astype(jnp.bfloat16)


def kernel(
    blocks,
    halves,
    q_ref,
    k_ref,
    v_ref,
    o_ref,
    k_buf,
    v_buf,
    own_sem,
    swap_send,
    swap_recv,
    prior_send,
    prior_recv,
    anchor_send,
    anchor_recv,
    relay_send,
    relay_recv,
):
    frames, rows, columns = q_ref.shape
    chunks = own_sem.shape[1]
    width = columns // chunks
    anchor_slot, prior_slot = frames, frames + 1
    z = lax.axis_index("frame")
    half = lax.axis_index("seq")
    later = (z + blocks - 1) // blocks
    ahead = {"frame": (z + 1) % blocks}
    first = z == 0
    sends_on = z < blocks - 1
    mine = pl.ds(pl.multiple_of(half * rows, rows), rows)
    sources, buffers = (k_ref, v_ref), (k_buf, v_buf)
    offsets = range(1, halves)

    def cols(c):
        return pl.ds(pl.multiple_of(c * width, LANES), width) if chunks > 1 else pl.ds(0, width)

    def sibling(j):
        return {"seq": (half + j) % halves}

    def remote(src, dst, send, recv, where):
        return pltpu.make_async_remote_copy(
            src_ref=src,
            dst_ref=dst,
            send_sem=send,
            recv_sem=recv,
            device_id=where,
            device_id_type=pl.DeviceIdType.MESH,
        )

    def own(i, c):
        return pltpu.make_async_copy(
            sources[i].at[pl.ds(0, frames - 1), :, cols(c)],
            buffers[i].at[pl.ds(0, frames - 1), mine, cols(c)],
            own_sem.at[i, c],
        )

    def swap(i, c, j):
        return remote(
            sources[i].at[pl.ds(0, frames - 1), :, cols(c)],
            buffers[i].at[pl.ds(0, frames - 1), mine, cols(c)],
            swap_send.at[i, c, j - 1],
            swap_recv.at[i, c, j - 1],
            sibling(j),
        )

    def prior(i, c):
        return remote(
            sources[i].at[frames - 1, :, cols(c)],
            buffers[i].at[prior_slot, mine, cols(c)],
            prior_send.at[i, c],
            prior_recv.at[i, c],
            ahead,
        )

    def anchor(i, c, root):
        here = buffers[i].at[anchor_slot, mine, cols(c)]
        return remote(
            sources[i].at[0, :, cols(c)] if root else here,
            here,
            anchor_send.at[i, c],
            anchor_recv.at[i, c],
            ahead,
        )

    def relay(which, i, c, j):
        here = buffers[i].at[anchor_slot + which, mine, cols(c)]
        return remote(
            here,
            here,
            relay_send.at[which, i, c, j - 1],
            relay_recv.at[which, i, c, j - 1],
            sibling(j),
        )

    barrier = pltpu.get_barrier_semaphore()

    @pl.when(sends_on)
    def _():
        pl.semaphore_signal(
            barrier, inc=1, device_id=ahead, device_id_type=pl.DeviceIdType.MESH
        )

    @pl.when(z > 0)
    def _():
        pl.semaphore_signal(
            barrier,
            inc=1,
            device_id={"frame": (z + blocks - 1) % blocks},
            device_id_type=pl.DeviceIdType.MESH,
        )

    for j in offsets:
        pl.semaphore_signal(
            barrier, inc=1, device_id=sibling(j), device_id_type=pl.DeviceIdType.MESH
        )
    pl.semaphore_wait(barrier, later + 1 - (z + 1) // blocks + halves - 1)

    @pl.when(first & sends_on)
    def _():
        @pl.loop(0, chunks)
        def _(c):
            for i in range(2):
                anchor(i, c, True).start()
            for i in range(2):
                prior(i, c).start()

    @pl.when((z > 0) & sends_on)
    def _():
        for i in range(2):
            prior(i, 0).start()

    @pl.loop(0, chunks)
    def _(c):
        for i in range(2):
            own(i, c).start()
            for j in offsets:
                swap(i, c, j).start()

    def receive(c):
        @pl.when(z > 0)
        def _():
            for i in range(2):
                anchor(i, c, False).wait_recv()

                @pl.when(sends_on)
                def _():
                    anchor(i, c, False).start()

                for j in offsets:
                    relay(0, i, c, j).start()

            @pl.when(sends_on & (c + 1 < chunks))
            def _():
                for i in range(2):
                    prior(i, c + 1).start()

            for i in range(2):
                prior(i, c).wait_recv()
                for j in offsets:
                    relay(1, i, c, j).start()

    def complete(c):
        for i in range(2):
            own(i, c).wait()
            for j in offsets:
                swap(i, c, j).wait_recv()

        @pl.when(z > 0)
        def _():
            for i in range(2):
                for j in offsets:
                    relay(0, i, c, j).wait_recv()
                    relay(1, i, c, j).wait_recv()

    block = min(rows, 512)
    per_frame = rows // block
    steps = frames * per_frame

    def compute(c, step):
        frame = step // per_frame
        opens = (frames - frame) // frames
        before = (frame - 1) * (1 - opens) + opens * later * prior_slot
        zero = later * anchor_slot
        at_rows = pl.ds(pl.multiple_of((step % per_frame) * block, block), block)
        for start in range(0, width, LANES):
            size = min(LANES, width - start)
            if chunks > 1:
                at = cols(c)
            else:
                at = pl.ds(start, size)
            o_ref[frame, at_rows, at] = attend_columns(
                q_ref[frame, at_rows, at],
                [k_buf[zero, :, at], k_buf[before, :, at]],
                [v_buf[zero, :, at], v_buf[before, :, at]],
            )

    receive(0)

    @pl.loop(0, chunks)
    def _(c):
        complete(c)

        @pl.loop(0, steps)
        def _(step):
            @pl.when((step == steps // 2) & (c + 1 < chunks))
            def _():
                receive(c + 1)

            compute(c, step)

    @pl.loop(0, chunks)
    def _(c):
        for i in range(2):
            for j in offsets:
                swap(i, c, j).wait_send()

            @pl.when(sends_on)
            def _():
                prior(i, c).wait_send()
                anchor(i, c, False).wait_send()

            @pl.when(z > 0)
            def _():
                for j in offsets:
                    relay(0, i, c, j).wait_send()
                    relay(1, i, c, j).wait_send()


def local(blocks, halves, queries, key_states, value_states):
    frames, rows, columns = queries.shape
    chunks = columns // LANES if columns % LANES == 0 else 1
    held = pltpu.VMEM((frames + 2, rows * halves, columns), queries.dtype)
    dma = pltpu.SemaphoreType.DMA
    plain = dma((2, chunks))
    across = dma((2, chunks, halves - 1))
    relays = dma((2, 2, chunks, halves - 1))
    anywhere = pl.BlockSpec(memory_space=pl.ANY)
    near = pl.BlockSpec(memory_space=pltpu.VMEM)
    return pl.pallas_call(
        functools.partial(kernel, blocks, halves),
        out_shape=jax.ShapeDtypeStruct(queries.shape, queries.dtype),
        in_specs=[near, anywhere, anywhere],
        out_specs=near,
        scratch_shapes=[
            held,
            held,
            plain,
            across,
            across,
            plain,
            plain,
            plain,
            plain,
            relays,
            relays,
        ],
        compiler_params=pltpu.CompilerParams(
            collective_id=0, has_side_effects=True, vmem_limit_bytes=56 * 1024 * 1024
        ),
    )(queries, key_states, value_states)


def solution(mesh):
    spec = P(("groups", "frame"), "seq", "head")
    body = functools.partial(local, mesh.shape["frame"], mesh.shape["seq"])
    return jax.shard_map(
        body, mesh=mesh, in_specs=(spec, spec, spec), out_specs=spec, check_vma=False
    )
```

```python
import functools

import jax
import jax.numpy as jnp
from jax import lax
from jax.experimental import pallas as pl
from jax.experimental.pallas import tpu as pltpu
from jax.sharding import PartitionSpec as P

HEAD_DIM = 64
LANES = 128
KEY_BLOCK = 512


def stack_heads(q):
    head_of_lane = lax.broadcasted_iota(jnp.int32, q.shape, 1) // HEAD_DIM
    scaled = q * jnp.asarray(HEAD_DIM**-0.5, q.dtype)
    return jnp.concatenate(
        [
            jnp.where(head_of_lane == h, scaled, jnp.zeros_like(scaled))
            for h in range(q.shape[1] // HEAD_DIM)
        ],
        0,
    )


def add_keys(stacked, keys, values, row_max, total):
    for k, v in zip(keys, values):
        for start in range(0, k.shape[0], KEY_BLOCK):
            k_part, v_part = k[start : start + KEY_BLOCK], v[start : start + KEY_BLOCK]
            summed = jnp.concatenate([v_part, jnp.ones_like(v_part)], 1)
            scores = lax.dot_general(
                stacked, k_part, (((1,), (1,)), ((), ())), preferred_element_type=jnp.float32
            )
            newer = jnp.max(scores, axis=1, keepdims=True)
            if row_max is not None:
                newer = jnp.maximum(row_max, newer)
            rounded = jnp.exp(scores - newer).astype(jnp.bfloat16)
            part = jnp.dot(rounded, summed, preferred_element_type=jnp.float32)
            total = part if row_max is None else total * jnp.exp(row_max - newer) + part
            row_max = newer
    return row_max, total


def finish(total, rows, width):
    out = total[:, :width] / total[:, width:]
    result = out[:rows]
    head_of_lane = lax.broadcasted_iota(jnp.int32, result.shape, 1) // HEAD_DIM
    for h in range(1, width // HEAD_DIM):
        result = jnp.where(head_of_lane == h, out[h * rows : (h + 1) * rows], result)
    return result.astype(jnp.bfloat16)


def early_chunks(chunks):
    return 3 if chunks > 3 else 0


def kernel(
    blocks,
    halves,
    q_ref,
    k_ref,
    v_ref,
    o_ref,
    k_buf,
    v_buf,
    own_sem,
    swap_send,
    swap_recv,
    prior_send,
    prior_recv,
    anchor_send,
    anchor_recv,
    relay_send,
    relay_recv,
    max_buf,
    sum_buf,
):
    frames, rows, columns = q_ref.shape
    chunks = own_sem.shape[1]
    width = columns // chunks
    anchor_slot, prior_slot = frames, frames + 1
    early = early_chunks(chunks)
    late = chunks - early
    z = lax.axis_index("frame")
    half = lax.axis_index("seq")
    later = (z + blocks - 1) // blocks
    ahead = {"frame": (z + 1) % blocks}
    first = z == 0
    sends_on = z < blocks - 1
    mine = pl.ds(pl.multiple_of(half * rows, rows), rows)
    sources, buffers = (k_ref, v_ref), (k_buf, v_buf)
    offsets = range(1, halves)

    def cols(c):
        return pl.ds(pl.multiple_of(c * width, LANES), width) if chunks > 1 else pl.ds(0, width)

    def sibling(j):
        return {"seq": (half + j) % halves}

    def remote(src, dst, send, recv, where):
        return pltpu.make_async_remote_copy(
            src_ref=src,
            dst_ref=dst,
            send_sem=send,
            recv_sem=recv,
            device_id=where,
            device_id_type=pl.DeviceIdType.MESH,
        )

    def own(i, c):
        return pltpu.make_async_copy(
            sources[i].at[pl.ds(0, frames - 1), :, cols(c)],
            buffers[i].at[pl.ds(0, frames - 1), mine, cols(c)],
            own_sem.at[i, c],
        )

    def swap(i, c, j):
        return remote(
            sources[i].at[pl.ds(0, frames - 1), :, cols(c)],
            buffers[i].at[pl.ds(0, frames - 1), mine, cols(c)],
            swap_send.at[i, c, j - 1],
            swap_recv.at[i, c, j - 1],
            sibling(j),
        )

    def prior(i, c):
        return remote(
            sources[i].at[frames - 1, :, cols(c)],
            buffers[i].at[prior_slot, mine, cols(c)],
            prior_send.at[i, c],
            prior_recv.at[i, c],
            ahead,
        )

    def anchor(i, c, root):
        here = buffers[i].at[anchor_slot, mine, cols(c)]
        return remote(
            sources[i].at[0, :, cols(c)] if root else here,
            here,
            anchor_send.at[i, c],
            anchor_recv.at[i, c],
            ahead,
        )

    def relay(which, i, c, j):
        here = buffers[i].at[anchor_slot + which, mine, cols(c)]
        return remote(
            here,
            here,
            relay_send.at[which, i, c, j - 1],
            relay_recv.at[which, i, c, j - 1],
            sibling(j),
        )

    barrier = pltpu.get_barrier_semaphore()

    @pl.when(sends_on)
    def _():
        pl.semaphore_signal(
            barrier, inc=1, device_id=ahead, device_id_type=pl.DeviceIdType.MESH
        )

    @pl.when(z > 0)
    def _():
        pl.semaphore_signal(
            barrier,
            inc=1,
            device_id={"frame": (z + blocks - 1) % blocks},
            device_id_type=pl.DeviceIdType.MESH,
        )

    for j in offsets:
        pl.semaphore_signal(
            barrier, inc=1, device_id=sibling(j), device_id_type=pl.DeviceIdType.MESH
        )
    pl.semaphore_wait(barrier, later + 1 - (z + 1) // blocks + halves - 1)

    @pl.when(first & sends_on)
    def _():
        @pl.loop(0, chunks)
        def _(c):
            for i in range(2):
                anchor(i, c, True).start()
            for i in range(2):
                prior(i, c).start()

    @pl.when((z > 0) & sends_on)
    def _():
        for i in range(2):
            prior(i, 0).start()

    @pl.loop(0, chunks)
    def _(turn):
        c = (turn + late) % chunks
        for i in range(2):
            own(i, c).start()
            for j in offsets:
                swap(i, c, j).start()

    def receive(c):
        @pl.when(z > 0)
        def _():
            for i in range(2):
                anchor(i, c, False).wait_recv()

                @pl.when(sends_on)
                def _():
                    anchor(i, c, False).start()

                for j in offsets:
                    relay(0, i, c, j).start()

            @pl.when(sends_on & (c + 1 < chunks))
            def _():
                for i in range(2):
                    prior(i, c + 1).start()

            for i in range(2):
                prior(i, c).wait_recv()
                for j in offsets:
                    relay(1, i, c, j).start()

    def complete_own(c):
        for i in range(2):
            own(i, c).wait()
            for j in offsets:
                swap(i, c, j).wait_recv()

    def complete_sent(c):
        @pl.when(z > 0)
        def _():
            for i in range(2):
                for j in offsets:
                    relay(0, i, c, j).wait_recv()
                    relay(1, i, c, j).wait_recv()

    zero = later * anchor_slot

    def whole(c, frame):
        opens = (frames - frame) // frames
        before = (frame - 1) * (1 - opens) + opens * later * prior_slot
        for start in range(0, width, LANES):
            size = min(LANES, width - start)
            at = cols(c) if chunks > 1 else pl.ds(start, size)
            _, total = add_keys(
                stack_heads(q_ref[frame, :, at]),
                [k_buf[zero, :, at], k_buf[before, :, at]],
                [v_buf[zero, :, at], v_buf[before, :, at]],
                None,
                None,
            )
            o_ref[frame, :, at] = finish(total, rows, size)

    def begin(c, frame):
        at = cols(c)
        row_max, total = add_keys(
            stack_heads(q_ref[frame, :, at]),
            [k_buf[frame - 1, :, at]],
            [v_buf[frame - 1, :, at]],
            None,
            None,
        )
        max_buf[c - late, frame - 1] = row_max
        sum_buf[c - late, frame - 1] = total

    def close(c, frame):
        at = cols(c)
        _, total = add_keys(
            stack_heads(q_ref[frame, :, at]),
            [k_buf[zero, :, at]],
            [v_buf[zero, :, at]],
            max_buf[c - late, frame - 1],
            sum_buf[c - late, frame - 1],
        )
        o_ref[frame, :, at] = finish(total, rows, width)

    if early:

        @pl.loop(0, early)
        def _(turn):
            complete_own(turn + late)

            @pl.loop(1, frames)
            def _(frame):
                begin(turn + late, frame)

            @pl.when((turn == z - 1) | ((turn == early - 1) & (z > early)))
            def _():
                receive(0)
    else:
        receive(0)

    @pl.loop(0, chunks)
    def _(c):
        @pl.when(c < late)
        def _():
            complete_own(c)

        complete_sent(c)

        @pl.loop(0, frames)
        def _(frame):
            @pl.when((frame == frames // 2) & (c + 1 < chunks))
            def _():
                receive(c + 1)

            if early:
                ready = (c >= late) & (frame > 0)

                @pl.when(ready)
                def _():
                    close(c, frame)

                @pl.when(jnp.logical_not(ready))
                def _():
                    whole(c, frame)
            else:
                whole(c, frame)

    @pl.loop(0, chunks)
    def _(c):
        for i in range(2):
            for j in offsets:
                swap(i, c, j).wait_send()

            @pl.when(sends_on)
            def _():
                prior(i, c).wait_send()
                anchor(i, c, False).wait_send()

            @pl.when(z > 0)
            def _():
                for j in offsets:
                    relay(0, i, c, j).wait_send()
                    relay(1, i, c, j).wait_send()


def local(blocks, halves, queries, key_states, value_states):
    frames, rows, columns = queries.shape
    chunks = columns // LANES if columns % LANES == 0 else 1
    held = pltpu.VMEM((frames + 2, rows * halves, columns), queries.dtype)
    dma = pltpu.SemaphoreType.DMA
    early = early_chunks(chunks)
    kept = (early, frames - 1, rows * LANES // HEAD_DIM) if early else (1, 1, 8)
    plain = dma((2, chunks))
    across = dma((2, chunks, halves - 1))
    relays = dma((2, 2, chunks, halves - 1))
    anywhere = pl.BlockSpec(memory_space=pl.ANY)
    near = pl.BlockSpec(memory_space=pltpu.VMEM)
    return pl.pallas_call(
        functools.partial(kernel, blocks, halves),
        out_shape=jax.ShapeDtypeStruct(queries.shape, queries.dtype),
        in_specs=[near, anywhere, anywhere],
        out_specs=near,
        scratch_shapes=[
            held,
            held,
            plain,
            across,
            across,
            plain,
            plain,
            plain,
            plain,
            relays,
            relays,
            pltpu.VMEM(kept + (1,), jnp.float32),
            pltpu.VMEM(kept + (2 * LANES,), jnp.float32),
        ],
        compiler_params=pltpu.CompilerParams(
            collective_id=0, has_side_effects=True, vmem_limit_bytes=56 * 1024 * 1024
        ),
    )(queries, key_states, value_states)


def solution(mesh):
    spec = P(("groups", "frame"), "seq", "head")
    body = functools.partial(local, mesh.shape["frame"], mesh.shape["seq"])
    return jax.shard_map(
        body, mesh=mesh, in_specs=(spec, spec, spec), out_specs=spec, check_vma=False
    )
```

```python
import functools

import jax
import jax.numpy as jnp
from jax import lax
from jax.experimental import pallas as pl
from jax.experimental.pallas import tpu as pltpu
from jax.sharding import PartitionSpec as P

HEAD_DIM = 64
LANES = 128
KEY_BLOCK = 512


def attend_columns(q, keys, values):
    rows, width = q.shape
    heads = width // HEAD_DIM
    head_of_lane = lax.broadcasted_iota(jnp.int32, q.shape, 1) // HEAD_DIM
    scaled = q * jnp.asarray(HEAD_DIM**-0.5, q.dtype)
    stacked = jnp.concatenate(
        [jnp.where(head_of_lane == h, scaled, jnp.zeros_like(scaled)) for h in range(heads)], 0
    )
    row_max = total = None
    for k, v in zip(keys, values):
        for start in range(0, k.shape[0], KEY_BLOCK):
            k_part, v_part = k[start : start + KEY_BLOCK], v[start : start + KEY_BLOCK]
            summed = jnp.concatenate([v_part, jnp.ones_like(v_part)], 1)
            scores = lax.dot_general(
                stacked, k_part, (((1,), (1,)), ((), ())), preferred_element_type=jnp.float32
            )
            newer = jnp.max(scores, axis=1, keepdims=True)
            if row_max is not None:
                newer = jnp.maximum(row_max, newer)
            rounded = jnp.exp(scores - newer).astype(jnp.bfloat16)
            part = jnp.dot(rounded, summed, preferred_element_type=jnp.float32)
            total = part if row_max is None else total * jnp.exp(row_max - newer) + part
            row_max = newer
    out = total[:, :width] / total[:, width:]
    result = out[:rows]
    for h in range(1, heads):
        result = jnp.where(head_of_lane == h, out[h * rows : (h + 1) * rows], result)
    return result.astype(jnp.bfloat16)


def kernel(
    blocks,
    halves,
    q_ref,
    k_ref,
    v_ref,
    o_ref,
    k_buf,
    v_buf,
    own_sem,
    swap_send,
    swap_recv,
    prior_send,
    prior_recv,
    anchor_send,
    anchor_recv,
    relay_send,
    relay_recv,
):
    frames, rows, columns = q_ref.shape
    chunks = own_sem.shape[1]
    width = columns // chunks
    anchor_slot, prior_slot = frames, frames + 1
    z = lax.axis_index("frame")
    half = lax.axis_index("seq")
    later = (z + blocks - 1) // blocks
    ahead = {"frame": (z + 1) % blocks}
    first = z == 0
    sends_on = z < blocks - 1
    mine = pl.ds(pl.multiple_of(half * rows, rows), rows)
    sources, buffers = (k_ref, v_ref), (k_buf, v_buf)
    offsets = range(1, halves)

    def cols(c):
        return pl.ds(pl.multiple_of(c * width, LANES), width) if chunks > 1 else pl.ds(0, width)

    def sibling(j):
        return {"seq": (half + j) % halves}

    def remote(src, dst, send, recv, where):
        return pltpu.make_async_remote_copy(
            src_ref=src,
            dst_ref=dst,
            send_sem=send,
            recv_sem=recv,
            device_id=where,
            device_id_type=pl.DeviceIdType.MESH,
        )

    def own(i, c):
        return pltpu.make_async_copy(
            sources[i].at[pl.ds(0, frames - 1), :, cols(c)],
            buffers[i].at[pl.ds(0, frames - 1), mine, cols(c)],
            own_sem.at[i, c],
        )

    def swap(i, c, j):
        return remote(
            sources[i].at[pl.ds(0, frames - 1), :, cols(c)],
            buffers[i].at[pl.ds(0, frames - 1), mine, cols(c)],
            swap_send.at[i, c, j - 1],
            swap_recv.at[i, c, j - 1],
            sibling(j),
        )

    def prior(i, c):
        return remote(
            sources[i].at[frames - 1, :, cols(c)],
            buffers[i].at[prior_slot, mine, cols(c)],
            prior_send.at[i, c],
            prior_recv.at[i, c],
            ahead,
        )

    def anchor(i, c, root):
        here = buffers[i].at[anchor_slot, mine, cols(c)]
        return remote(
            sources[i].at[0, :, cols(c)] if root else here,
            here,
            anchor_send.at[i, c],
            anchor_recv.at[i, c],
            ahead,
        )

    def relay(which, i, c, j):
        here = buffers[i].at[anchor_slot + which, mine, cols(c)]
        return remote(
            here,
            here,
            relay_send.at[which, i, c, j - 1],
            relay_recv.at[which, i, c, j - 1],
            sibling(j),
        )

    barrier = pltpu.get_barrier_semaphore()

    @pl.when(sends_on)
    def _():
        pl.semaphore_signal(
            barrier, inc=1, device_id=ahead, device_id_type=pl.DeviceIdType.MESH
        )

    @pl.when(z > 0)
    def _():
        pl.semaphore_signal(
            barrier,
            inc=1,
            device_id={"frame": (z + blocks - 1) % blocks},
            device_id_type=pl.DeviceIdType.MESH,
        )

    for j in offsets:
        pl.semaphore_signal(
            barrier, inc=1, device_id=sibling(j), device_id_type=pl.DeviceIdType.MESH
        )
    pl.semaphore_wait(barrier, later + 1 - (z + 1) // blocks + halves - 1)

    def send_first(c):
        for i in range(2):
            anchor(i, c, True).start()
        for i in range(2):
            prior(i, c).start()

    @pl.when(first & sends_on)
    def _():
        send_first(0)

    @pl.when((z > 0) & sends_on)
    def _():
        for i in range(2):
            prior(i, 0).start()

    @pl.loop(0, chunks)
    def _(c):
        for i in range(2):
            own(i, c).start()
            for j in offsets:
                swap(i, c, j).start()

    def receive(c):
        @pl.when(z > 0)
        def _():
            for i in range(2):
                anchor(i, c, False).wait_recv()

                @pl.when(sends_on)
                def _():
                    anchor(i, c, False).start()

                for j in offsets:
                    relay(0, i, c, j).start()

            @pl.when(sends_on & (c + 1 < chunks))
            def _():
                for i in range(2):
                    prior(i, c + 1).start()

            for i in range(2):
                prior(i, c).wait_recv()
                for j in offsets:
                    relay(1, i, c, j).start()

    def complete(c):
        for i in range(2):
            own(i, c).wait()
            for j in offsets:
                swap(i, c, j).wait_recv()

        @pl.when(z > 0)
        def _():
            for i in range(2):
                for j in offsets:
                    relay(0, i, c, j).wait_recv()
                    relay(1, i, c, j).wait_recv()

    block = min(rows, 512)
    per_frame = rows // block
    steps = frames * per_frame

    def compute(c, step):
        frame = step // per_frame
        opens = (frames - frame) // frames
        before = (frame - 1) * (1 - opens) + opens * later * prior_slot
        zero = later * anchor_slot
        at_rows = pl.ds(pl.multiple_of((step % per_frame) * block, block), block)
        for start in range(0, width, LANES):
            size = min(LANES, width - start)
            if chunks > 1:
                at = cols(c)
            else:
                at = pl.ds(start, size)
            o_ref[frame, at_rows, at] = attend_columns(
                q_ref[frame, at_rows, at],
                [k_buf[zero, :, at], k_buf[before, :, at]],
                [v_buf[zero, :, at], v_buf[before, :, at]],
            )

    receive(0)

    @pl.loop(0, chunks)
    def _(c):
        complete(c)

        @pl.loop(0, steps)
        def _(step):
            @pl.when((step == steps // 2 - 1 + later) & (c + 1 < chunks))
            def _():
                receive(c + 1)

                @pl.when(first & sends_on)
                def _():
                    send_first(c + 1)

            compute(c, step)

    @pl.loop(0, chunks)
    def _(c):
        for i in range(2):
            for j in offsets:
                swap(i, c, j).wait_send()

            @pl.when(sends_on)
            def _():
                prior(i, c).wait_send()
                anchor(i, c, False).wait_send()

            @pl.when(z > 0)
            def _():
                for j in offsets:
                    relay(0, i, c, j).wait_send()
                    relay(1, i, c, j).wait_send()


def local(blocks, halves, queries, key_states, value_states):
    frames, rows, columns = queries.shape
    chunks = columns // LANES if columns % LANES == 0 else 1
    held = pltpu.VMEM((frames + 2, rows * halves, columns), queries.dtype)
    dma = pltpu.SemaphoreType.DMA
    plain = dma((2, chunks))
    across = dma((2, chunks, halves - 1))
    relays = dma((2, 2, chunks, halves - 1))
    anywhere = pl.BlockSpec(memory_space=pl.ANY)
    near = pl.BlockSpec(memory_space=pltpu.VMEM)
    return pl.pallas_call(
        functools.partial(kernel, blocks, halves),
        out_shape=jax.ShapeDtypeStruct(queries.shape, queries.dtype),
        in_specs=[near, anywhere, anywhere],
        out_specs=near,
        scratch_shapes=[
            held,
            held,
            plain,
            across,
            across,
            plain,
            plain,
            plain,
            plain,
            relays,
            relays,
        ],
        compiler_params=pltpu.CompilerParams(
            collective_id=0, has_side_effects=True, vmem_limit_bytes=56 * 1024 * 1024
        ),
    )(queries, key_states, value_states)


def solution(mesh):
    spec = P(("groups", "frame"), "seq", "head")
    body = functools.partial(local, mesh.shape["frame"], mesh.shape["seq"])
    return jax.shard_map(
        body, mesh=mesh, in_specs=(spec, spec, spec), out_specs=spec, check_vma=False
    )
```
